128 devices in a mesh: grp: 2 (over core), row: 16 (over y, x), col: 4 (over z).
Axes of the slice: x: 4, y: 4, z: 4, core: 2. Of those that a mesh axis runs over, the one named last changes fastest.
Arguments:
- root_inverse: bfloat16 [12288, 12288], P(('grp', 'row'), 'col'), may hold values from -0.0546875 to 0.0546875
- child_inverse: bfloat16 [2, 8192, 8192], P('grp', 'row', 'col'), may hold values from -0.0625 to 0.0625
- coupling: bfloat16 [2, 1536, 8192], P('grp', 'col', 'row'), may hold values from -0.0625 to 0.0625
- child_weights: bfloat16 [2, 8192], P('grp', 'col'), may hold values from 0.5 to 2
- root_weights: bfloat16 [12288], P('col'), may hold values from 0.5 to 2
- parent_blocks: int32 [2, 12], replicated, may hold values from 0 to 95, as said below
Outputs:
- grad_root: bfloat16 [12288, 12288], P(('grp', 'row'), 'col')
- grad_child: bfloat16 [2, 8192, 8192], P('grp', 'row', 'col')
- grad_coupling: bfloat16 [2, 1536, 8192], P('grp', 'col', 'row')
The draws below stay inside these ranges and needn't reach their ends.
Inputs may be any that keep to these rules, and one draw needn't show every extreme that they name: `parent_blocks`: within one child the 12 blocks are distinct; child 0 always names block 0 and block 12288 // 128 - 1; the two children may share blocks.
All inputs are finite; a program needn't handle non-finite values.
Results may differ from the reference program's by a relative error of at most 0.0059.
Values may be sent and summed in bfloat16 or wider, within the bound.
A program may use at most 128 MiB of HBM per device.

```python
import jax
import jax.numpy as jnp

NR = 12288
NC = 8192
BW = 128
MB = 12
M = 1536


def draw_parent_blocks(key, part):
    total = NR // BW
    inner = jax.random.permutation(jax.random.fold_in(key, 11), total - 2)[:MB - 2] + 1
    first = jnp.concatenate([jnp.zeros((1,), jnp.int32), inner.astype(jnp.int32), jnp.full((1,), total - 1, jnp.int32)])
    second = jax.random.permutation(jax.random.fold_in(key, 12), total)[:MB].astype(jnp.int32)
    return jnp.stack([first, second]).astype(jnp.int32)


def shard_levels(own_key, shape, shards, least, largest):
    def one(axis_at, shards_of):
        steps = jax.random.uniform(jax.random.fold_in(jax.random.fold_in(own_key, 6), axis_at), (shards_of,), jnp.float32, least / len(shards), largest / len(shards))
        return jnp.repeat(jnp.exp(steps), shape[axis_at] // shards_of).reshape((-1,) + (1,) * (len(shape) - axis_at - 1))

    loudness = one(*shards[0])
    for cut in shards[1:]:
        loudness = loudness * one(*cut)
    return loudness


def noise(key, shape, deviation, limit, pieces=(), held_as=jnp.bfloat16):
    array = deviation * jax.random.normal(key, shape, jnp.float32)
    if pieces:
        array = array * shard_levels(key, shape, pieces, -0.22, 0.18)
    return jnp.clip(array, -limit, limit).astype(held_as)


def setup_inputs(seed: int = 0) -> dict:
    seeds = jax.random.split(jax.random.key(seed), 7)
    return {
        "root_inverse": noise(seeds[0], (NR, NR), NR ** -0.5, 0.0546875, ((0, 32), (1, 4))),
        "child_inverse": noise(seeds[1], (2, NC, NC), NC ** -0.5, 0.0625, ((0, 2), (1, 16), (2, 4))),
        "coupling": noise(seeds[2], (2, M, NC), NC ** -0.5, 0.0625, ((0, 2), (1, 4), (2, 16))),
        "child_weights": jnp.clip(0.5 + 1.5 * jax.random.uniform(seeds[3], (2, NC), jnp.float32) ** shard_levels(seeds[3], (2, NC), ((0, 2), (1, 4)), -0.2, 0.2), 0.5, 2.0).astype(jnp.bfloat16),
        "root_weights": jnp.clip(0.5 + 1.5 * jax.random.uniform(seeds[4], (NR,), jnp.float32) ** shard_levels(seeds[4], (NR,), ((0, 4),), -0.2, 0.2), 0.5, 2.0).astype(jnp.bfloat16),
        "parent_blocks": draw_parent_blocks(jax.random.fold_in(seeds[6], 71), 0),
    }


def matmul(left, right):
    return jnp.dot(left.astype(jnp.float32), right.astype(jnp.float32), preferred_element_type=jnp.float32)


def reference(root_inverse, child_inverse, coupling, child_weights, root_weights, parent_blocks):
    offsets = jnp.arange(BW, dtype=jnp.int32)
    grad_root = 2.0 * root_inverse.astype(jnp.float32) * root_weights.astype(jnp.float32)[None, :]
    grads_factor = []
    grads_links = []
    for child in range(2):
        columns = (parent_blocks[child][:, None].astype(jnp.int32) * BW + offsets[None, :]).reshape(-1).astype(jnp.int32)
        selected = jnp.take(root_inverse, columns, axis=1)
        margin = matmul(selected.T, selected).astype(jnp.bfloat16)
        factor = child_inverse[child]
        links = coupling[child]
        weights = child_weights[child].astype(jnp.float32)
        solved = matmul(links, factor).astype(jnp.bfloat16)
        scaled = (solved.astype(jnp.float32) * weights[None, :]).astype(jnp.bfloat16)
        adjoint = matmul(scaled, solved.T).astype(jnp.bfloat16)
        lifted = matmul(selected, adjoint).astype(jnp.bfloat16)
        grad_root = grad_root.at[:, columns].add(2.0 * lifted.astype(jnp.float32))
        pulled = (2.0 * matmul(margin, solved) * weights[None, :]).astype(jnp.bfloat16)
        grads_links.append(matmul(pulled, factor.T).astype(jnp.bfloat16))
        grad_factor = matmul(links.T, pulled) + 2.0 * factor.astype(jnp.float32) * weights[None, :]
        grads_factor.append(grad_factor.astype(jnp.bfloat16))
    return grad_root.astype(jnp.bfloat16), jnp.stack(grads_factor), jnp.stack(grads_links)
```

```python
import functools

import jax
import jax.numpy as jnp
from jax import lax
from jax.experimental import pallas as pl
from jax.experimental.pallas import tpu as pltpu
from jax.sharding import PartitionSpec as P

BW = 128
MESH = pl.DeviceIdType.MESH
VMEM = pl.BlockSpec(memory_space=pltpu.VMEM)
SMEM = pl.BlockSpec(memory_space=pltpu.SMEM)
F32 = jnp.float32
BF16 = jnp.bfloat16


def ring(i, step):
    return lax.rem(i + step, 4)


class Place:
    def __init__(self):
        row = lax.axis_index("row")
        self.x = lax.rem(row, 4)
        self.y = row // 4
        self.z = lax.axis_index("col")
        self.core = lax.axis_index("grp")
        self.sibling = {"grp": 1 - self.core}
        self.axes = {
            "x": (self.x, [{"row": self.y * 4 + ring(self.x, s)} for s in (1, 3)]),
            "y": (self.y, [{"row": ring(self.y, s) * 4 + self.x} for s in (1, 3)]),
            "z": (self.z, [{"col": ring(self.z, s)} for s in (1, 3)]),
        }

    def meet(self, with_sibling):
        barrier = pltpu.get_barrier_semaphore()
        others = [dev for _, devs in self.axes.values() for dev in devs]
        if with_sibling:
            others.append(self.sibling)
        for dev in others:
            pl.semaphore_signal(barrier, inc=1, device_id=dev, device_id_type=MESH)
        pl.semaphore_wait(barrier, len(others))


class Net:
    def __init__(self, send, recv):
        self.send, self.recv, self.made = send, recv, []

    def copy(self, src, dst, dev):
        at = len(self.made)
        made = pltpu.make_async_remote_copy(
            src_ref=src,
            dst_ref=dst,
            send_sem=self.send.at[at],
            recv_sem=self.recv.at[at],
            device_id=dev,
            device_id_type=MESH,
        )
        self.made.append(made)
        return made

    def drain(self):
        for made in self.made:
            made.wait_send()


class Gather:
    def __init__(self, net, axis, view, own=None):
        me, (right, left) = axis
        lo, hi = ring(me, 3), ring(me, 1)
        own = view(me, None) if own is None else own
        self.first = [net.copy(own, view(me, None), right), net.copy(own, view(me, None), left)]
        self.second = [
            net.copy(view(lo, 0), view(lo, 0), right),
            net.copy(view(hi, 1), view(hi, 1), left),
        ]

    def start(self):
        for copy in self.first:
            copy.start()

    def relay(self):
        for came, goes in zip(self.first, self.second):
            came.wait_recv()
            goes.start()

    def finish(self):
        for copy in self.second:
            copy.wait_recv()


def add_to(ref, other):
    if len(ref.shape) == 2:
        ref[...] = (ref[...].astype(F32) + other[...].astype(F32)).astype(BF16)
        return

    def body(i, _):
        ref[i] = (ref[i].astype(F32) + other[i].astype(F32)).astype(BF16)
        return 0

    lax.fori_loop(0, ref.shape[0], body, 0)


class Scatter:
    def __init__(self, net, axis, view, relay, fin):
        me, (right, left) = axis
        up, down, far = ring(me, 1), ring(me, 3), ring(me, 2)
        self.far = [net.copy(view(far, 0), relay(0), right), net.copy(view(far, 1), relay(1), left)]
        self.near = [
            net.copy(view(up, 1), fin(0, 1), right),
            net.copy(view(down, 0), fin(1, 0), left),
        ]
        self.last = [
            net.copy(relay(0), fin(0, 0), right),
            net.copy(relay(1), fin(1, 1), left),
        ]
        self.adds = [(relay(0), view(up, 0)), (relay(1), view(down, 1))]

    def start(self):
        for copy in self.far + self.near:
            copy.start()

    def relay(self):
        for came, goes, add in zip(self.far, self.last, self.adds):
            came.wait_recv()
            add_to(*add)
            goes.start()

    def finish(self):
        for copy in self.near + self.last:
            copy.wait_recv()


def total(*terms):
    out = terms[0].astype(F32)
    for term in terms[1:]:
        out = out + term.astype(F32)
    return out.astype(BF16)


class GridGather:
    def __init__(self, net, place, buf):
        rows, cols = buf.shape[2:]
        cut = (cols // BW + 1) // 2 * BW
        wide = [pl.ds(0, cut), pl.ds(cut, cols - cut)]
        pair = [pl.ds(0, 2), pl.ds(2, 2)]
        top, low = pl.ds(0, rows // 2), pl.ds(rows // 2, rows // 2)
        x, y = place.x, place.y

        def x_first(i, part):
            return buf.at[y, i, top, :] if part is None else buf.at[y, i, top, wide[part]]

        def y_second(i, part):
            return buf.at[i, :, top, :] if part is None else buf.at[i, pair[part], top, :]

        def y_first(i, part):
            return buf.at[i, x, low, :] if part is None else buf.at[i, x, low, wide[part]]

        def x_second(i, part):
            return buf.at[:, i, low, :] if part is None else buf.at[pair[part], i, low, :]

        self.one = [
            Gather(net, place.axes["x"], x_first),
            Gather(net, place.axes["y"], y_first),
        ]
        self.two = [
            Gather(net, place.axes["y"], y_second),
            Gather(net, place.axes["x"], x_second),
        ]

    def start(self):
        for ring_ in self.one:
            ring_.start()

    def relay(self):
        for ring_ in self.one:
            ring_.relay()

    def turn(self):
        for before, after in zip(self.one, self.two):
            before.finish()
            after.start()

    def relay_two(self):
        for ring_ in self.two:
            ring_.relay()

    def finish(self):
        for ring_ in self.two:
            ring_.finish()


def grid_scatter_scratch(rows, cols):
    half = rows // 2
    cut = (cols // BW + 1) // 2 * BW
    return [
        pltpu.VMEM((2, 2, 2, half, cols), BF16),
        pltpu.VMEM((2, 2, 4, half, cols), BF16),
        pltpu.VMEM((2, 4, half, cols), BF16),
        pltpu.VMEM((2, half, cut), BF16),
        pltpu.VMEM((2, half, cols - cut), BF16),
        pltpu.VMEM((2, 2, half, cols), BF16),
    ]


class GridScatter:
    def __init__(self, net, place, buf, scratch):
        far, fin, mid, far_a, far_b, fin_two = scratch
        rows, cols = buf.shape[2:]
        self.half = half = rows // 2
        cut = (cols // BW + 1) // 2 * BW
        wide = [pl.ds(0, cut), pl.ds(cut, cols - cut)]
        pair = [pl.ds(0, 2), pl.ds(2, 2)]
        top, low = pl.ds(0, half), pl.ds(half, half)
        self.place, self.buf, self.fin, self.mid, self.fin_two = place, buf, fin, mid, fin_two
        far_two = [far_a, far_b]

        def views(h):
            def first(i, part):
                if h == 0:
                    return buf.at[i, pair[part], top, :]
                return buf.at[pair[part], i, low, :]

            def second(i, part):
                return mid.at[h, i, :, wide[part]]

            one = (
                first,
                lambda side: far.at[h, side],
                lambda side, part: fin.at[h, side, pair[part]],
            )
            two = (
                second,
                lambda side: far_two[side].at[h],
                lambda side, part: fin_two.at[h, side, :, wide[part]],
            )
            return one, two

        names = [("y", "x"), ("x", "y")]
        self.one, self.two = [], []
        for h in range(2):
            one, two = views(h)
            self.one.append(Scatter(net, place.axes[names[h][0]], *one))
            self.two.append(Scatter(net, place.axes[names[h][1]], *two))

    def start(self):
        for ring_ in self.one:
            ring_.start()

    def relay(self):
        for ring_ in self.one:
            ring_.relay()

    def turn(self):
        for h in range(2):
            self.one[h].finish()
            rows = pl.ds(h * self.half, self.half)

            def body(i, _):
                own = (
                    self.buf[self.place.y, i, rows, :]
                    if h == 0
                    else self.buf[i, self.place.x, rows, :]
                )
                self.mid[h, i] = total(own, self.fin[h, 0, i], self.fin[h, 1, i])
                return 0

            lax.fori_loop(0, 4, body, 0)
            self.two[h].start()

    def relay_two(self):
        for ring_ in self.two:
            ring_.relay()

    def finish(self, out):
        for h in range(2):
            self.two[h].finish()
            own = self.mid[h, self.place.x if h == 0 else self.place.y]
            rows = pl.ds(h * self.half, self.half)
            out[rows, :] = total(own, self.fin_two[h, 0], self.fin_two[h, 1])


def dot(left, right, dims=((1,), (0,))):
    return lax.dot_general(left, right, (dims, ((), ())), preferred_element_type=F32)


def pick_kernel(at_ref, have_ref, w_ref, out_ref):
    for child in range(2):
        for j in range(12):
            block = w_ref[:, pl.ds(pl.multiple_of(at_ref[child, j] * BW, BW), BW)]
            mine = block.astype(F32) * have_ref[child, j].astype(F32)
            out_ref[j // 3, child, :, pl.ds((j % 3) * BW, BW)] = mine.astype(BF16)


SENDS_ONE = 54


def first_kernel(
    pk, l_ref, f_ref, la, sa, sel, p, g_far, g_fin, own, s0, s1, s2, s3, s4, s5, send, recv
):
    place = Place()
    z = place.z
    place.meet(False)
    net = Net(send, recv)
    half = [pl.ds(0, 192), pl.ds(192, 192)]
    links = Gather(
        net,
        place.axes["z"],
        lambda i, part: la.at[i] if part is None else la.at[i, half[part]],
        own=l_ref,
    )
    picked = Scatter(
        net,
        place.axes["z"],
        lambda i, part: pk.at[i, part],
        lambda side: g_far.at[side],
        lambda side, part: g_fin.at[side, part],
    )
    spread = Gather(
        net,
        place.axes["z"],
        lambda i, part: sel.at[i] if part is None else sel.at[i, part],
    )
    reduced = GridScatter(net, place, p, [s0, s1, s2, s3, s4, s5])
    solved = GridGather(net, place, sa)

    def fill(q, source):
        def body(t, _):
            cols = pl.ds(pl.multiple_of(t * 512, 512), 512)
            part = dot(source[...], f_ref[:, cols]).astype(BF16)
            for k in range(4):
                p[q, k, :, cols] = part[96 * k : 96 * k + 96]
            return 0

        lax.fori_loop(0, 4, body, 0)

    links.start()
    la[z] = l_ref[...]
    fill(z, l_ref)
    links.relay()
    picked.start()
    fill(ring(z, 1), la.at[ring(z, 1)])
    fill(ring(z, 3), la.at[ring(z, 3)])
    links.finish()
    fill(ring(z, 2), la.at[ring(z, 2)])
    reduced.start()
    reduced.relay()
    picked.relay()
    reduced.turn()
    picked.finish()
    for child in range(2):
        sel[z, child] = total(pk[z, child], g_fin[0, child], g_fin[1, child])
    spread.start()
    reduced.relay_two()
    reduced.finish(own)
    sa[place.y, place.x] = own[...]
    solved.start()
    solved.relay()
    solved.turn()
    spread.relay()
    solved.relay_two()
    spread.finish()
    solved.finish()
    net.drain()


SENDS_TWO = 78


def second_kernel(
    sel, sa, f_ref, w_ref, pa, lf, out, mo, m_in, m4, block, mr, ap, d_far, d_fin, aj, gp, k_far,
    k_fin, s0, s1, s2, s3, s4, s5, send, recv,
):
    place = Place()
    x, y, z, core = place.x, place.y, place.z, place.core
    place.meet(True)
    net = Net(send, recv)
    half = [pl.ds(0, 48), pl.ds(48, 48)]
    tall = [pl.ds(0, 192), pl.ds(192, 192)]
    other = 1 - core
    swap = net.copy(mo, m_in, place.sibling)
    margin = GridScatter(net, place, m4, [s0, s1, s2, s3, s4, s5])
    margin_row = Gather(
        net,
        place.axes["z"],
        lambda i, part: mr.at[i] if part is None else mr.at[i, half[part]],
    )
    adjoint = Scatter(
        net,
        place.axes["z"],
        lambda i, part: ap.at[i, half[part]],
        lambda side: d_far.at[side],
        lambda side, part: d_fin.at[side, half[part]],
    )
    adjoint_all = GridGather(net, place, aj.at[core])
    adjoint_swap = net.copy(aj.at[core], aj.at[core], place.sibling)
    pulled = GridGather(net, place, pa)
    lifted = Gather(
        net,
        place.axes["z"],
        lambda i, part: lf.at[i] if part is None else lf.at[i, part],
    )
    grad = Scatter(
        net,
        place.axes["z"],
        lambda i, part: gp.at[i, tall[part]],
        lambda side: k_far.at[side],
        lambda side, part: k_fin.at[side, tall[part]],
    )

    def cross(q, _):
        part = dot(sel[q, other], sel[z, other], ((0,), (0,))).astype(BF16)
        for k in range(4):
            mo[q, k] = part[96 * k : 96 * k + 96]
        return 0

    lax.fori_loop(0, 4, cross, 0)
    swap.start()
    scaled = (sa[y, x].astype(F32) * w_ref[...]).astype(BF16)

    def adjoint_rows(q, _):
        right = sa[q].reshape(384, 2048)
        ap[q] = dot(scaled, right, ((1,), (1,))).astype(BF16)
        return 0

    lax.fori_loop(0, 4, adjoint_rows, 0)
    adjoint.start()
    swap.wait_recv()

    def same(q, _):
        part = dot(sel[q, core], sel[z, core], ((0,), (0,)))
        for k in range(4):
            m4[q, k] = (part[96 * k : 96 * k + 96] + m_in[q, k].astype(F32)).astype(BF16)
        return 0

    lax.fori_loop(0, 4, same, 0)
    margin.start()
    adjoint.relay()
    margin.relay()
    adjoint.finish()
    aj[core, y, x] = total(ap[z], d_fin[0], d_fin[1])
    margin.turn()
    adjoint_all.start()
    margin.relay_two()
    margin.finish(block)
    mr[z] = block[...]
    margin_row.start()
    adjoint_all.relay()
    margin_row.relay()
    margin_row.finish()

    def pull(t, _):
        cols = pl.ds(pl.multiple_of(t * 512, 512), 512)
        part = jnp.zeros((96, 512), F32)
        for q in range(4):
            part = part + dot(mr[q], sa[q, :, :, cols].reshape(384, 512))
        pa[y, x, :, cols] = (2.0 * part * w_ref[:, cols]).astype(BF16)
        return 0

    lax.fori_loop(0, 4, pull, 0)
    pulled.start()
    adjoint_all.turn()
    pulled.relay()
    adjoint_all.relay_two()
    adjoint_all.finish()
    adjoint_swap.start()

    def lift(child):
        part = jnp.zeros((384, 384), F32)
        for q in range(4):
            part = part + dot(sel[q, child], aj[child, q].reshape(384, 384))
        lf[z, child] = part.astype(BF16)

    lift(core)
    pulled.turn()
    adjoint_swap.wait_recv()
    lift(other)
    lifted.start()
    pulled.relay_two()
    lifted.relay()
    pulled.finish()

    def project(q, _):
        gp[q] = dot(pa[q].reshape(384, 2048), f_ref[...], ((1,), (1,))).astype(BF16)
        return 0

    lax.fori_loop(0, 4, project, 0)
    grad.start()
    grad.relay()
    lifted.finish()
    grad.finish()
    out[...] = total(gp[z], k_fin[0], k_fin[1])
    net.drain()


def place_kernel(at_ref, have_ref, w_ref, s_ref, lf_ref, out_ref):
    def body(b, _):
        cols = pl.ds(pl.multiple_of(b * BW, BW), BW)
        value = 2.0 * w_ref[:, cols].astype(F32) * s_ref[:, cols]
        for child in range(2):
            j = at_ref[child, b]
            third = pl.ds(pl.multiple_of(lax.rem(j, 3) * BW, BW), BW)
            part = lf_ref[j // 3, child, :, third].astype(F32)
            value = value + 2.0 * part * have_ref[child, b].astype(F32)
        out_ref[:, cols] = value.astype(BF16)
        return 0

    lax.fori_loop(0, 24, body, 0)


def shape(*dims):
    return jax.ShapeDtypeStruct(dims, BF16)


def local(root_inverse, child_inverse, coupling, child_weights, root_weights, parent_blocks):
    col_index = lax.axis_index("col")
    root_rows, root_cols = root_inverse.shape
    local_blocks = root_cols // BW
    offset = parent_blocks - col_index * local_blocks
    have = ((offset >= 0) & (offset < local_blocks)).astype(jnp.int32)
    at = jnp.clip(offset, 0, local_blocks - 1)
    match = offset[:, None, :] == jnp.arange(local_blocks, dtype=jnp.int32)[None, :, None]
    back_have = jnp.any(match, axis=2).astype(jnp.int32)
    back_at = jnp.sum(match * jnp.arange(12, dtype=jnp.int32)[None, None, :], axis=2)

    picked = pl.pallas_call(
        pick_kernel,
        out_shape=shape(4, 2, root_rows, 384),
        in_specs=[SMEM, SMEM, VMEM],
        out_specs=VMEM,
        name="pick",
    )(at, have, root_inverse)

    factor = child_inverse[0]
    weights = child_weights[0].astype(F32)[None, :]
    links_all, solved_all, selected = pl.pallas_call(
        first_kernel,
        out_shape=(shape(4, 384, 512), shape(4, 4, 96, 2048), shape(4, 2, 384, 384)),
        in_specs=[VMEM] * 3,
        out_specs=(VMEM,) * 3,
        scratch_shapes=[
            pltpu.VMEM((4, 4, 96, 2048), BF16),
            pltpu.VMEM((2, 384, 384), BF16),
            pltpu.VMEM((2, 2, 384, 384), BF16),
            pltpu.VMEM((96, 2048), BF16),
            *grid_scatter_scratch(96, 2048),
            pltpu.SemaphoreType.DMA((SENDS_ONE,)),
            pltpu.SemaphoreType.DMA((SENDS_ONE,)),
        ],
        compiler_params=pltpu.CompilerParams(collective_id=0, has_side_effects=True),
        name="solve",
    )(picked, coupling[0], factor)

    pulled_all, lifted_all, grad_links = pl.pallas_call(
        second_kernel,
        out_shape=(shape(4, 4, 96, 2048), shape(4, 2, 384, 384), shape(384, 512)),
        in_specs=[VMEM] * 4,
        out_specs=(VMEM,) * 3,
        scratch_shapes=[
            pltpu.VMEM((4, 4, 96, 384), BF16),
            pltpu.VMEM((4, 4, 96, 384), BF16),
            pltpu.VMEM((4, 4, 96, 384), BF16),
            pltpu.VMEM((96, 384), BF16),
            pltpu.VMEM((4, 96, 384), BF16),
            pltpu.VMEM((4, 96, 384), BF16),
            pltpu.VMEM((2, 48, 384), BF16),
            pltpu.VMEM((2, 96, 384), BF16),
            pltpu.VMEM((2, 4, 4, 96, 384), BF16),
            pltpu.VMEM((4, 384, 512), BF16),
            pltpu.VMEM((2, 192, 512), BF16),
            pltpu.VMEM((2, 384, 512), BF16),
            *grid_scatter_scratch(96, 384),
            pltpu.SemaphoreType.DMA((SENDS_TWO,)),
            pltpu.SemaphoreType.DMA((SENDS_TWO,)),
        ],
        compiler_params=pltpu.CompilerParams(collective_id=1, has_side_effects=True),
        name="pull",
    )(selected, solved_all, factor, weights)

    grad_root = pl.pallas_call(
        place_kernel,
        out_shape=shape(root_rows, root_cols),
        in_specs=[SMEM, SMEM, VMEM, VMEM, VMEM],
        out_specs=VMEM,
        name="place",
    )(back_at, back_have, root_inverse, root_weights.astype(F32)[None, :], lifted_all)

    grad_factor = jnp.dot(
        links_all.reshape(1536, 512).T,
        pulled_all.reshape(1536, 2048),
        preferred_element_type=F32,
    )
    grad_factor = (grad_factor + 2.0 * factor.astype(F32) * weights).astype(BF16)
    return (grad_root, grad_factor[None], grad_links[None])


def solution(mesh):
    return jax.shard_map(
        local,
        mesh=mesh,
        in_specs=(
            P(("grp", "row"), "col"),
            P("grp", "row", "col"),
            P("grp", "col", "row"),
            P("grp", "col"),
            P("col"),
            P(),
        ),
        out_specs=(P(("grp", "row"), "col"), P("grp", "row", "col"), P("grp", "col", "row")),
        check_vma=False,
    )
```
